512 devices in a mesh: lang: 16 (over z_lo, y), bulk: 32 (over z_hi, x, core).
Axes of the slice: x: 4, y: 8, z: 8 (z_hi: 4, z_lo: 2; z = z_hi * 2 + z_lo), core: 2. Of those that a mesh axis runs over, the one named last changes fastest.
Arguments:
- sources: bfloat16 [524288, 1024], P(('lang', 'bulk')), may hold values from -24 to 24
- lang_ids: int32 [4096], P(('lang', 'bulk')), may hold values from 0 to 15
- centers: float32 [16, 1024], replicated, may hold values from -3 to 3
- targets: bfloat16 [1024, 1024], P('bulk'), may hold values from -12 to 12
Outputs:
- hubness: float32 [1024], P('bulk')
- source_logsum: float32 [524288], P(('lang', 'bulk'))
- source_match: float32 [524288], P(('lang', 'bulk'))
The draws below stay inside these ranges and needn't reach their ends.
All inputs are finite; a program needn't handle non-finite values.
Results may differ from the reference program's by a relative error of at most 0.0043.
Values may be sent and summed in bfloat16 or wider, within the bound.
A program may use at most 64 MiB of HBM per device.

```python
import math
import jax
import jax.numpy as jnp
from jax import lax

D = 1024
LANGS = 16
ROWBLK = 128
S = 524288
T_SIZE = 1024


def spread_scales(key, count):
    return jnp.exp(jax.random.uniform(key, (count, 1), jnp.float32, math.log(0.35), math.log(3.5)))


def draw_sources(key, part):
    row_index = jnp.arange(S, dtype=jnp.float32)[:, None]
    scales = spread_scales(jax.random.fold_in(key, 21), S)
    base = jax.random.normal(jax.random.fold_in(key, 23), (S, D), jnp.float32)
    values = base * scales * jnp.power(3.0, row_index / S - 0.5)
    return jnp.clip(values, -24.0, 24.0).astype(jnp.bfloat16)


def draw_targets(key, part):
    scales = spread_scales(jax.random.fold_in(key, 31), T_SIZE)
    base = jax.random.normal(jax.random.fold_in(key, 33), (T_SIZE, D), jnp.float32)
    values = base * scales
    return jnp.clip(values, -12.0, 12.0).astype(jnp.bfloat16)


def set_ends(values, key, least, high):
    dims = values.shape
    index_at = [jax.random.randint(jax.random.fold_in(key, axis), (), 0, dims[axis]) for axis in range(len(dims))]
    values = values.at[tuple(index_at)].set(least)
    longest = dims.index(max(dims))
    index_at[longest] = (index_at[longest] + 1) % dims[longest]
    return values.at[tuple(index_at)].set(high)


def bell_draw(key, shape, deviation, most, held_as=jnp.bfloat16):
    drawn = deviation * jax.random.normal(key, shape, jnp.float32)
    return jnp.clip(drawn, min=-most, max=most).astype(held_as)


def setup_inputs(seed: int = 0) -> dict:
    streams_of = jax.random.split(jax.random.key(seed), 5)
    sources = draw_sources(jax.random.fold_in(streams_of[4], 71), 0)
    lang_ids = set_ends(jax.random.randint(streams_of[1], (S // ROWBLK,), 0, LANGS), jax.random.fold_in(streams_of[1], 1), 0, LANGS - 1).astype(jnp.int32)
    centers = bell_draw(streams_of[2], (LANGS, D), 0.5, 3.0, jnp.float32)
    targets = draw_targets(jax.random.fold_in(streams_of[4], 71), 0)
    return {"sources": sources, "lang_ids": lang_ids, "centers": centers, "targets": targets}


def reference(sources, lang_ids, centers, targets):
    chosen = (lang_ids[:, None] == jnp.arange(LANGS, dtype=jnp.int32)[None, :]).astype(jnp.float32)
    offsets = jnp.dot(chosen, centers, precision=lax.Precision.HIGHEST, preferred_element_type=jnp.float32)
    grouped = sources.astype(jnp.float32).reshape(S // ROWBLK, ROWBLK, D)
    centered = (grouped - offsets[:, None, :]).reshape(S, D).astype(jnp.bfloat16)
    temper = D ** -0.5
    piece_rows = math.gcd(S, 8192)
    stacked = centered.reshape(S // piece_rows, piece_rows, D)

    def score_block(source_block):
        products = lax.dot_general(targets, source_block, (((1,), (1,)), ((), ())), preferred_element_type=jnp.float32)
        return products * temper

    def hub_step(carried, source_block):
        tile = score_block(source_block)
        upper = jnp.maximum(carried[0], jnp.max(tile, axis=1))
        weight = carried[1] * jnp.exp(carried[0] - upper) + jnp.sum(jnp.exp(tile - upper[:, None]), axis=1)
        return (upper, weight), None

    start_state = (jnp.full((T_SIZE,), -jnp.inf, jnp.float32), jnp.zeros((T_SIZE,), jnp.float32))
    (peak_all, weight_all), unused = lax.scan(hub_step, start_state, stacked)
    hubness = peak_all + jnp.log(weight_all)

    def read_block(source_block):
        tile = score_block(source_block)
        adjusted = 2.0 * tile - hubness[:, None]
        upper = jnp.max(adjusted, axis=0)
        weights = jnp.exp(adjusted - upper[None, :])
        summed = jnp.sum(weights, axis=0)
        return upper + jnp.log(summed), jnp.sum(weights * tile, axis=0) / summed

    logsum_parts, match_parts = lax.map(read_block, stacked)
    return hubness, logsum_parts.reshape(S), match_parts.reshape(S)
```

```python
import functools

import jax
import jax.numpy as jnp
from jax import lax
from jax.experimental import pallas as pl
from jax.experimental.pallas import tpu as pltpu
from jax.sharding import PartitionSpec as P

MESH = pl.DeviceIdType.MESH
SENDS = (4, 3, 5, 2, 6, 1, 7)


def kernel(
    rowblk,
    ids_ref, centers_ref, targets_ref, sources_ref,
    hub_ref, logsum_ref, match_ref,
    raw, centered, held, scores, hubs, parts,
    load_sem,
    z_send, z_recv, x_send, x_recv, c_send, c_recv,
    r_send, r_recv,
):
    lang = lax.axis_index("lang")
    bulk = lax.axis_index("bulk")
    zl, y = lang // 8, lang % 8
    k, x, c = bulk // 8, (bulk // 2) % 4, bulk % 2
    low = bulk % 8
    z = k * 2 + zl
    width = centers_ref.shape[1]
    temper = width ** (-0.5)
    nblk = raw.shape[0]
    piece_rows = targets_ref.shape[0]
    half = piece_rows // 2

    def at_bulk(kk, xx, cc):
        return (lang, kk * 8 + xx * 2 + cc)

    def slot(dk, dx, cc):
        return cc * 16 + lax.rem(k + dk, 4) * 4 + lax.rem(x + dx, 4)

    up_k = at_bulk(lax.rem(k + 1, 4), x, c)
    down_k = at_bulk(lax.rem(k + 3, 4), x, c)
    up_x = at_bulk(k, lax.rem(x + 1, 4), c)
    down_x = at_bulk(k, lax.rem(x + 3, 4), c)
    sibling = at_bulk(k, x, 1 - c)

    stage_me = (low, y, z)
    stage_peer = (
        lambda j: (lang, k * 8 + lax.rem(low + j, 8)),
        lambda j: (zl * 8 + lax.rem(y + j, 8), bulk),
        lambda j: (lax.rem(z + j, 2) * 8 + y, (lax.rem(z + j, 8) // 2) * 8 + low),
    )

    loads = []
    for b in range(nblk):
        load = pltpu.make_async_copy(
            sources_ref.at[pl.ds(b * rowblk, rowblk), :], raw.at[b], load_sem.at[b]
        )
        load.start()
        loads.append(load)

    barrier = pltpu.get_barrier_semaphore()
    for stage in range(3):
        for j in range(1, 8):
            pl.semaphore_signal(
                barrier, inc=1, device_id=stage_peer[stage](j), device_id_type=MESH
            )
    pl.semaphore_wait(barrier, 21)

    started = []

    def send(src, dst, send_sem, recv_sem, device):
        copy = pltpu.make_async_remote_copy(
            src_ref=src, dst_ref=dst, send_sem=send_sem, recv_sem=recv_sem,
            device_id=device, device_id_type=MESH,
        )
        copy.start()
        started.append(copy)

    def arrived(dst, send_sem, recv_sem):
        pltpu.make_async_remote_copy(
            src_ref=dst, dst_ref=dst, send_sem=send_sem, recv_sem=recv_sem,
            device_id=sibling, device_id_type=MESH,
        ).wait_recv()

    def piece(dk, dx):
        return held.at[slot(dk, dx, c)]

    def part(ref, which):
        return ref.at[pl.ds(which * half, half), :]

    def to_sibling(dk, dx, src=None):
        dst = piece(dk, dx)
        send(dst if src is None else src, dst, c_send.at[dk, dx], c_recv.at[dk, dx], sibling)

    def along_x(dk, src=None):
        dst = piece(dk, 0)
        src = dst if src is None else src
        send(src, dst, x_send.at[dk, 0], x_recv.at[dk, 0], up_x)
        send(src, dst, x_send.at[dk, 1], x_recv.at[dk, 1], down_x)
        to_sibling(dk, 0, src)

    def relay_x(dk):
        left = piece(dk, 3)
        arrived(left, x_send.at[dk, 0], x_recv.at[dk, 0])
        send(part(left, 0), part(left, 0), x_send.at[dk, 2], x_recv.at[dk, 2], up_x)
        to_sibling(dk, 3)
        right = piece(dk, 1)
        arrived(right, x_send.at[dk, 1], x_recv.at[dk, 1])
        send(part(right, 1), part(right, 1), x_send.at[dk, 3], x_recv.at[dk, 3], down_x)
        to_sibling(dk, 1)

    def finish_x(dk):
        far = piece(dk, 2)
        arrived(part(far, 0), x_send.at[dk, 2], x_recv.at[dk, 2])
        arrived(part(far, 1), x_send.at[dk, 3], x_recv.at[dk, 3])
        to_sibling(dk, 2)

    own = piece(0, 0)
    send(targets_ref, own, z_send.at[0], z_recv.at[0], up_k)
    send(targets_ref, own, z_send.at[1], z_recv.at[1], down_k)
    along_x(0, targets_ref)
    held[slot(0, 0, c)] = targets_ref[...]

    for b in range(nblk):
        loads[b].wait()
        offset = centers_ref[pl.ds(ids_ref[b], 1), :]
        centered[b] = (raw[b].astype(jnp.float32) - offset).astype(jnp.bfloat16)

    below = piece(3, 0)
    arrived(below, z_send.at[0], z_recv.at[0])
    send(part(below, 0), part(below, 0), z_send.at[2], z_recv.at[2], up_k)
    along_x(3)
    above = piece(1, 0)
    arrived(above, z_send.at[1], z_recv.at[1])
    send(part(above, 1), part(above, 1), z_send.at[3], z_recv.at[3], down_k)
    along_x(1)
    relay_x(0)
    relay_x(3)
    relay_x(1)
    across = piece(2, 0)
    arrived(part(across, 0), z_send.at[2], z_recv.at[2])
    arrived(part(across, 1), z_send.at[3], z_recv.at[3])
    along_x(2)
    finish_x(0)
    relay_x(2)
    finish_x(3)
    finish_x(1)
    finish_x(2)
    for dk in range(4):
        for dx in range(4):
            arrived(held.at[slot(dk, dx, 1 - c)], c_send.at[dk, dx], c_recv.at[dk, dx])

    count = held.shape[0] * piece_rows

    def score_step(b, carried):
        peak, weight = carried
        tile = lax.dot_general(
            centered[b], held[...].reshape(count, width), (((1,), (1,)), ((), ())),
            preferred_element_type=jnp.float32,
        ) * temper
        scores[b] = tile
        grouped = tile.reshape(rowblk // 8, 8, count)
        new_peak = jnp.maximum(peak, jnp.max(grouped, axis=0))
        weight = weight * jnp.exp(peak - new_peak) + jnp.sum(
            jnp.exp(grouped - new_peak[None]), axis=0
        )
        return new_peak, weight

    peak, weight = lax.fori_loop(
        0, nblk, score_step,
        (jnp.full((8, count), -jnp.inf, jnp.float32), jnp.zeros((8, count), jnp.float32)),
    )
    top = jnp.max(peak, axis=0, keepdims=True)
    hub = top + jnp.log(jnp.sum(weight * jnp.exp(peak - top), axis=0, keepdims=True))
    for j in range(8):
        hubs[0, pl.ds(j, 1), :] = hub[:, j * 128:(j + 1) * 128]

    for stage in range(3):
        me = stage_me[stage]
        for j in SENDS:
            send(
                hubs.at[stage], parts.at[stage, me], r_send.at[stage, j], r_recv.at[stage, j],
                stage_peer[stage](j),
            )
        parts[stage, me] = hubs[stage]
        for j in range(1, 8):
            arrived(
                parts.at[stage, lax.rem(me + 8 - j, 8)], r_send.at[stage, j], r_recv.at[stage, j]
            )
        every = parts[stage]
        most = jnp.max(every, axis=0)
        hubs[stage + 1] = most + jnp.log(jnp.sum(jnp.exp(every - most[None]), axis=0))

    hub_row = jnp.concatenate([hubs[3, pl.ds(j, 1), :] for j in range(8)], axis=1)
    where_own = slot(0, 0, c)
    lanes = hubs[3, pl.ds(where_own // 4, 1), :]
    quarter = where_own % 4
    mine = jnp.zeros((1, piece_rows), jnp.float32)
    for q in range(4):
        mine = jnp.where(quarter == q, lanes[:, q * piece_rows:(q + 1) * piece_rows], mine)
    hub_ref[...] = mine

    eye = lax.broadcasted_iota(jnp.int32, (rowblk, rowblk), 0) == lax.broadcasted_iota(
        jnp.int32, (rowblk, rowblk), 1
    )

    def read_step(b, unused):
        tile = scores[b]
        adjusted = 2.0 * tile - hub_row
        most = jnp.max(adjusted, axis=1, keepdims=True)
        weights = jnp.exp(adjusted - most)
        summed = jnp.sum(weights, axis=1, keepdims=True)
        matched = jnp.sum(weights * tile, axis=1, keepdims=True)
        logsum = most + jnp.log(summed)
        match = matched / summed
        logsum_ref[pl.ds(b, 1), :] = jnp.sum(jnp.where(eye, logsum, 0.0), axis=0, keepdims=True)
        match_ref[pl.ds(b, 1), :] = jnp.sum(jnp.where(eye, match, 0.0), axis=0, keepdims=True)
        return unused

    lax.fori_loop(0, nblk, read_step, 0)
    for copy in started:
        copy.wait_send()


def per_device(sources, lang_ids, centers, targets):
    rows, width = sources.shape
    nblk = lang_ids.shape[0]
    rowblk = rows // nblk
    piece_rows = targets.shape[0]
    count = 32 * piece_rows
    vmem = pl.BlockSpec(memory_space=pltpu.VMEM)
    dma = pltpu.SemaphoreType.DMA
    hub, logsum, match = pl.pallas_call(
        functools.partial(kernel, rowblk),
        out_shape=(
            jax.ShapeDtypeStruct((1, piece_rows), jnp.float32),
            jax.ShapeDtypeStruct((nblk, rowblk), jnp.float32),
            jax.ShapeDtypeStruct((nblk, rowblk), jnp.float32),
        ),
        in_specs=[
            pl.BlockSpec(memory_space=pltpu.SMEM), vmem, vmem,
            pl.BlockSpec(memory_space=pl.ANY),
        ],
        out_specs=(vmem, vmem, vmem),
        scratch_shapes=[
            pltpu.VMEM((nblk, rowblk, width), jnp.bfloat16),
            pltpu.VMEM((nblk, rowblk, width), jnp.bfloat16),
            pltpu.VMEM((32, piece_rows, width), jnp.bfloat16),
            pltpu.VMEM((nblk, rowblk, count), jnp.float32),
            pltpu.VMEM((4, 8, count // 8), jnp.float32),
            pltpu.VMEM((3, 8, 8, count // 8), jnp.float32),
            dma((nblk,)),
            dma((4,)), dma((4,)),
            dma((4, 4)), dma((4, 4)),
            dma((4, 4)), dma((4, 4)),
            dma((3, 8)), dma((3, 8)),
        ],
        compiler_params=pltpu.CompilerParams(
            collective_id=0, has_side_effects=True, vmem_limit_bytes=48 * 1024 * 1024
        ),
        name="csls",
    )(lang_ids, centers, targets, sources)
    return hub.reshape(piece_rows), logsum.reshape(rows), match.reshape(rows)


def solution(mesh):
    in_specs = (P(("lang", "bulk"), None), P(("lang", "bulk")), P(), P("bulk", None))
    out_specs = (P("bulk"), P(("lang", "bulk")), P(("lang", "bulk")))
    return jax.shard_map(
        per_device, mesh=mesh, in_specs=in_specs, out_specs=out_specs, check_vma=False
    )
```

```python
import functools

import jax
import jax.numpy as jnp
from jax import lax
from jax.experimental import pallas as pl
from jax.experimental.pallas import tpu as pltpu
from jax.sharding import PartitionSpec as P

MESH = pl.DeviceIdType.MESH
SENDS = (4, 3, 5, 2, 6, 1, 7)
FAR_DIRECT = (0, 1, 2, 3)


def kernel(
    rowblk,
    ids_hbm, centers_hbm, targets_hbm, sources_hbm,
    hub_ref, logsum_ref, match_ref,
    ids, centers, raw, centered, held, scores, hubs, parts,
    load_sem, small_sem,
    z_send, z_recv, x_send, x_recv, y_send, y_recv, c_send, c_recv,
    r_send, r_recv,
):
    lang = lax.axis_index("lang")
    bulk = lax.axis_index("bulk")
    zl, y = lang // 8, lang % 8
    k, x, c = bulk // 8, (bulk // 2) % 4, bulk % 2
    low = bulk % 8
    z = k * 2 + zl
    nblk, _, width = raw.shape
    temper = width ** (-0.5)
    piece_rows = held.shape[1]
    half = piece_rows // 2
    group = 8 * piece_rows
    mine = y % 2

    def at_bulk(kk, xx, cc):
        return (lang, kk * 8 + xx * 2 + cc)

    def slot(dk, dx, cc):
        return lax.rem(k + dk, 4) * 8 + lax.rem(x + dx, 4) * 2 + cc

    up_k = at_bulk(lax.rem(k + 1, 4), x, c)
    down_k = at_bulk(lax.rem(k + 3, 4), x, c)
    up_x = at_bulk(k, lax.rem(x + 1, 4), c)
    down_x = at_bulk(k, lax.rem(x + 3, 4), c)
    far_x = at_bulk(k, lax.rem(x + 2, 4), c)
    up_y = (zl * 8 + lax.rem(y + 1, 8), bulk)
    down_y = (zl * 8 + lax.rem(y + 7, 8), bulk)
    sibling = at_bulk(k, x, 1 - c)

    stage_me = (low, y, z)
    stage_peer = (
        lambda j: (lang, k * 8 + lax.rem(low + j, 8)),
        lambda j: (zl * 8 + lax.rem(y + j, 8), bulk),
        lambda j: (lax.rem(z + j, 2) * 8 + y, (lax.rem(z + j, 8) // 2) * 8 + low),
    )

    barrier = pltpu.get_barrier_semaphore()
    for stage in range(3):
        for j in range(1, 8):
            pl.semaphore_signal(
                barrier, inc=1, device_id=stage_peer[stage](j), device_id_type=MESH
            )

    own = held.at[bulk]
    own_load = pltpu.make_async_copy(targets_hbm, own, small_sem.at[0])
    ids_load = pltpu.make_async_copy(ids_hbm, ids, small_sem.at[1])
    centers_load = pltpu.make_async_copy(centers_hbm, centers, small_sem.at[2])
    own_load.start()
    ids_load.start()
    centers_load.start()
    loads = []
    for b in range(nblk):
        load = pltpu.make_async_copy(
            sources_hbm.at[pl.ds(b * rowblk, rowblk), :], raw.at[b], load_sem.at[b]
        )
        load.start()
        loads.append(load)

    own_load.wait()
    pl.semaphore_wait(barrier, 21)

    started = []

    def send(ref, send_sem, recv_sem, device):
        copy = pltpu.make_async_remote_copy(
            src_ref=ref, dst_ref=ref, send_sem=send_sem, recv_sem=recv_sem,
            device_id=device, device_id_type=MESH,
        )
        copy.start()
        started.append(copy)

    def arrived(ref, send_sem, recv_sem):
        pltpu.make_async_remote_copy(
            src_ref=ref, dst_ref=ref, send_sem=send_sem, recv_sem=recv_sem,
            device_id=sibling, device_id_type=MESH,
        ).wait_recv()

    def rows(dk, dx, which, cc=c):
        return held.at[slot(dk, dx, cc), pl.ds(pl.multiple_of(which * half, half), half), :]

    def lanes(dk, dx, which, side):
        return held.at[
            slot(dk, dx, cc=c),
            pl.ds(pl.multiple_of(which * half, half), half),
            pl.ds(side * (width // 2), width // 2),
        ]

    def share(dk, dx):
        ref = rows(dk, dx, mine)
        send(
            ref, y_send.at[dk, dx], y_recv.at[dk, dx],
            up_y if (dk + dx) % 2 == 0 else down_y,
        )
        send(ref, c_send.at[0, dk, dx], c_recv.at[0, dk, dx], sibling)

    def along_x(dk):
        ref = rows(dk, 0, mine)
        send(ref, x_send.at[dk, 0], x_recv.at[dk, 0], up_x)
        send(ref, x_send.at[dk, 1], x_recv.at[dk, 1], down_x)
        if dk in FAR_DIRECT:
            send(ref, x_send.at[dk, 2], x_recv.at[dk, 2], far_x)

    def relay_x(dk):
        arrived(rows(dk, 3, mine), x_send.at[dk, 0], x_recv.at[dk, 0])
        if dk not in FAR_DIRECT:
            send(lanes(dk, 3, mine, 0), x_send.at[dk, 2], x_recv.at[dk, 2], up_x)
        share(dk, 3)
        arrived(rows(dk, 1, mine), x_send.at[dk, 1], x_recv.at[dk, 1])
        if dk not in FAR_DIRECT:
            send(lanes(dk, 1, mine, 1), x_send.at[dk, 3], x_recv.at[dk, 3], down_x)
        share(dk, 1)

    def finish_x(dk):
        if dk in FAR_DIRECT:
            arrived(rows(dk, 2, mine), x_send.at[dk, 2], x_recv.at[dk, 2])
        else:
            arrived(lanes(dk, 2, mine, 0), x_send.at[dk, 2], x_recv.at[dk, 2])
            arrived(lanes(dk, 2, mine, 1), x_send.at[dk, 3], x_recv.at[dk, 3])
        share(dk, 2)

    def from_y(dk, dxs=(0, 3, 1, 2)):
        for dx in dxs:
            if (dk, dx) == (0, 0):
                continue
            ref = rows(dk, dx, 1 - mine)
            arrived(ref, y_send.at[dk, dx], y_recv.at[dk, dx])
            send(ref, c_send.at[1, dk, dx], c_recv.at[1, dk, dx], sibling)

    def from_sibling(dk):
        for dx in range(4):
            if (dk, dx) == (0, 0):
                arrived(held.at[slot(0, 0, 1 - c)], c_send.at[0, 0, 0], c_recv.at[0, 0, 0])
                continue
            arrived(rows(dk, dx, mine, 1 - c), c_send.at[0, dk, dx], c_recv.at[0, dk, dx])
            arrived(rows(dk, dx, 1 - mine, 1 - c), c_send.at[1, dk, dx], c_recv.at[1, dk, dx])

    def score(dk):
        first = lax.rem(k + dk, 4) * 8

        def score_step(b, carried):
            peak, weight = carried
            tile = lax.dot_general(
                centered[b], held[pl.ds(first, 8)].reshape(group, width),
                (((1,), (1,)), ((), ())), preferred_element_type=jnp.float32,
            ) * temper
            scores[dk, b] = tile
            grouped = tile.reshape(tile.shape[0] // 8, 8, group)
            new_peak = jnp.maximum(peak, jnp.max(grouped, axis=0))
            weight = weight * jnp.exp(peak - new_peak) + jnp.sum(
                jnp.exp(grouped - new_peak[None]), axis=0
            )
            return new_peak, weight

        peak, weight = lax.fori_loop(
            0, nblk, score_step,
            (jnp.full((8, group), -jnp.inf, jnp.float32), jnp.zeros((8, group), jnp.float32)),
        )
        top = jnp.max(peak, axis=0, keepdims=True)
        hub = top + jnp.log(jnp.sum(weight * jnp.exp(peak - top), axis=0, keepdims=True))
        for j in range(group // 128):
            hubs[0, pl.ds(lax.rem(k + dk, 4) * (group // 128) + j, 1), :] = hub[
                :, j * 128:(j + 1) * 128
            ]

    send(rows(0, 0, mine), z_send.at[0], z_recv.at[0], up_k)
    send(rows(0, 0, mine), z_send.at[1], z_recv.at[1], down_k)
    along_x(0)
    send(own, c_send.at[0, 0, 0], c_recv.at[0, 0, 0], sibling)

    ids_load.wait()
    centers_load.wait()
    for b in range(nblk):
        loads[b].wait()
        offset = centers[pl.ds(ids[b], 1), :]
        centered[b] = (raw[b].astype(jnp.float32) - offset).astype(jnp.bfloat16)

    relay_x(0)
    arrived(rows(3, 0, mine), z_send.at[0], z_recv.at[0])
    send(lanes(3, 0, mine, 0), z_send.at[2], z_recv.at[2], up_k)
    along_x(3)
    share(3, 0)
    arrived(rows(1, 0, mine), z_send.at[1], z_recv.at[1])
    send(lanes(1, 0, mine, 1), z_send.at[3], z_recv.at[3], down_k)
    along_x(1)
    share(1, 0)
    finish_x(0)
    relay_x(3)
    relay_x(1)
    from_y(0)
    arrived(lanes(2, 0, mine, 0), z_send.at[2], z_recv.at[2])
    arrived(lanes(2, 0, mine, 1), z_send.at[3], z_recv.at[3])
    along_x(2)
    share(2, 0)
    finish_x(3)
    finish_x(1)
    from_sibling(0)
    score(0)
    relay_x(2)
    from_y(3)
    from_y(1)
    finish_x(2)
    from_sibling(3)
    score(3)
    from_y(2)
    from_sibling(1)
    score(1)
    from_sibling(2)
    score(2)

    for stage in range(3):
        me = stage_me[stage]
        for j in SENDS:
            copy = pltpu.make_async_remote_copy(
                src_ref=hubs.at[stage], dst_ref=parts.at[stage, me],
                send_sem=r_send.at[stage, j], recv_sem=r_recv.at[stage, j],
                device_id=stage_peer[stage](j), device_id_type=MESH,
            )
            copy.start()
            started.append(copy)
        parts[stage, me] = hubs[stage]
        for j in range(1, 8):
            arrived(
                parts.at[stage, lax.rem(me + 8 - j, 8)], r_send.at[stage, j], r_recv.at[stage, j]
            )
        every = parts[stage]
        most = jnp.max(every, axis=0)
        hubs[stage + 1] = most + jnp.log(jnp.sum(jnp.exp(every - most[None]), axis=0))

    line = hubs[3, pl.ds(bulk // 4, 1), :]
    quarter = bulk % 4
    own_hub = jnp.zeros((1, piece_rows), jnp.float32)
    for q in range(4):
        own_hub = jnp.where(quarter == q, line[:, q * piece_rows:(q + 1) * piece_rows], own_hub)
    hub_ref[...] = own_hub

    hub_rows = [
        jnp.concatenate(
            [
                hubs[3, pl.ds(lax.rem(k + dk, 4) * (group // 128) + j, 1), :]
                for j in range(group // 128)
            ],
            axis=1,
        )
        for dk in range(4)
    ]
    eye = lax.broadcasted_iota(jnp.int32, (rowblk, rowblk), 0) == lax.broadcasted_iota(
        jnp.int32, (rowblk, rowblk), 1
    )

    def read_step(b, unused):
        tiles = [scores[dk, b] for dk in range(4)]
        adjusted = [2.0 * tiles[dk] - hub_rows[dk] for dk in range(4)]
        most = functools.reduce(jnp.maximum, adjusted)
        most = jnp.max(most, axis=1, keepdims=True)
        weights = [jnp.exp(adjusted[dk] - most) for dk in range(4)]
        summed = jnp.sum(sum(weights), axis=1, keepdims=True)
        matched = jnp.sum(
            sum(weights[dk] * tiles[dk] for dk in range(4)), axis=1, keepdims=True
        )
        logsum = most + jnp.log(summed)
        match = matched / summed
        logsum_ref[pl.ds(b, 1), :] = jnp.sum(jnp.where(eye, logsum, 0.0), axis=0, keepdims=True)
        match_ref[pl.ds(b, 1), :] = jnp.sum(jnp.where(eye, match, 0.0), axis=0, keepdims=True)
        return unused

    lax.fori_loop(0, nblk, read_step, 0)
    for copy in started:
        copy.wait_send()


def hand_out(hub_in, logsum_in, match_in, hub_out, logsum_out, match_out, sems):
    copies = [
        pltpu.make_async_copy(src, dst, sems.at[i])
        for i, (src, dst) in enumerate(
            ((hub_in, hub_out), (logsum_in, logsum_out), (match_in, match_out))
        )
    ]
    for copy in copies:
        copy.start()
    for copy in copies:
        copy.wait()


def per_device(sources, lang_ids, centers, targets):
    rows, width = sources.shape
    nblk = lang_ids.shape[0]
    rowblk = rows // nblk
    piece_rows = targets.shape[0]
    count = 32 * piece_rows
    vmem = pl.BlockSpec(memory_space=pltpu.VMEM)
    dma = pltpu.SemaphoreType.DMA
    hub, logsum, match = pl.pallas_call(
        functools.partial(kernel, rowblk),
        out_shape=(
            jax.ShapeDtypeStruct((1, piece_rows), jnp.float32),
            jax.ShapeDtypeStruct((nblk, rowblk), jnp.float32),
            jax.ShapeDtypeStruct((nblk, rowblk), jnp.float32),
        ),
        in_specs=[pl.BlockSpec(memory_space=pltpu.HBM)] * 4,
        out_specs=(vmem, vmem, vmem),
        scratch_shapes=[
            pltpu.SMEM((nblk,), jnp.int32),
            pltpu.VMEM(centers.shape, jnp.float32),
            pltpu.VMEM((nblk, rowblk, width), jnp.bfloat16),
            pltpu.VMEM((nblk, rowblk, width), jnp.bfloat16),
            pltpu.VMEM((32, piece_rows, width), jnp.bfloat16),
            pltpu.VMEM((4, nblk, rowblk, count // 4), jnp.float32),
            pltpu.VMEM((4, 8, count // 8), jnp.float32),
            pltpu.VMEM((3, 8, 8, count // 8), jnp.float32),
            dma((nblk,)), dma((3,)),
            dma((4,)), dma((4,)),
            dma((4, 4)), dma((4, 4)),
            dma((4, 4)), dma((4, 4)),
            dma((2, 4, 4)), dma((2, 4, 4)),
            dma((3, 8)), dma((3, 8)),
        ],
        compiler_params=pltpu.CompilerParams(
            collective_id=0, has_side_effects=True, vmem_limit_bytes=67043328
        ),
        name="csls",
    )(lang_ids, centers, targets, sources)
    hub, logsum, match = pl.pallas_call(
        hand_out,
        out_shape=tuple(jax.ShapeDtypeStruct(a.shape, a.dtype) for a in (hub, logsum, match)),
        in_specs=[pl.BlockSpec(memory_space=pl.ANY)] * 3,
        out_specs=[pl.BlockSpec(memory_space=pltpu.VMEM)] * 3,
        scratch_shapes=[dma((3,))],
        name="hand_out",
    )(hub, logsum, match)
    return hub.reshape(piece_rows), logsum.reshape(rows), match.reshape(rows)


def solution(mesh):
    in_specs = (P(("lang", "bulk"), None), P(("lang", "bulk")), P(), P("bulk", None))
    out_specs = (P("bulk"), P(("lang", "bulk")), P(("lang", "bulk")))
    return jax.shard_map(
        per_device, mesh=mesh, in_specs=in_specs, out_specs=out_specs, check_vma=False
    )
```

```python
import functools

import jax
import jax.numpy as jnp
from jax import lax
from jax.experimental import pallas as pl
from jax.experimental.pallas import tpu as pltpu
from jax.sharding import PartitionSpec as P

MESH = pl.DeviceIdType.MESH
SENDS = (4, 3, 5, 2, 6, 1, 7)
FAR_DIRECT = (0, 1, 2, 3)
SPAN = 4


def kernel(
    rowblk,
    ids_hbm, centers_hbm, targets_hbm, sources_hbm,
    hub_ref, logsum_ref, match_ref,
    ids, centers, raw, centered, held, scores, hubs, parts,
    load_sem, small_sem,
    z_send, z_recv, x_send, x_recv, y_send, y_recv, c_send, c_recv,
    r_send, r_recv,
):
    lang = lax.axis_index("lang")
    bulk = lax.axis_index("bulk")
    zl, y = lang // 8, lang % 8
    k, x, c = bulk // 8, (bulk // 2) % 4, bulk % 2
    low = bulk % 8
    z = k * 2 + zl
    nblk, _, width = raw.shape
    temper = width ** (-0.5)
    piece_rows = held.shape[1]
    half = piece_rows // 2
    group = 8 * piece_rows
    mine = y % 2

    def at_bulk(kk, xx, cc):
        return (lang, kk * 8 + xx * 2 + cc)

    def slot(dk, dx, cc):
        return lax.rem(k + dk, 4) * 8 + lax.rem(x + dx, 4) * 2 + cc

    up_k = at_bulk(lax.rem(k + 1, 4), x, c)
    down_k = at_bulk(lax.rem(k + 3, 4), x, c)
    up_x = at_bulk(k, lax.rem(x + 1, 4), c)
    down_x = at_bulk(k, lax.rem(x + 3, 4), c)
    far_x = at_bulk(k, lax.rem(x + 2, 4), c)
    up_y = (zl * 8 + lax.rem(y + 1, 8), bulk)
    down_y = (zl * 8 + lax.rem(y + 7, 8), bulk)
    sibling = at_bulk(k, x, 1 - c)

    stage_me = (low, y, z)
    stage_peer = (
        lambda j: (lang, k * 8 + lax.rem(low + j, 8)),
        lambda j: (zl * 8 + lax.rem(y + j, 8), bulk),
        lambda j: (lax.rem(z + j, 2) * 8 + y, (lax.rem(z + j, 8) // 2) * 8 + low),
    )

    barrier = pltpu.get_barrier_semaphore()
    for stage in range(3):
        for j in range(1, 8):
            pl.semaphore_signal(
                barrier, inc=1, device_id=stage_peer[stage](j), device_id_type=MESH
            )

    own = held.at[bulk]
    own_load = pltpu.make_async_copy(targets_hbm, own, small_sem.at[0])
    ids_load = pltpu.make_async_copy(ids_hbm, ids, small_sem.at[1])
    centers_load = pltpu.make_async_copy(centers_hbm, centers, small_sem.at[2])
    own_load.start()
    ids_load.start()
    centers_load.start()
    loads = []
    for b in range(nblk):
        load = pltpu.make_async_copy(
            sources_hbm.at[pl.ds(b * rowblk, rowblk), :], raw.at[b], load_sem.at[b]
        )
        load.start()
        loads.append(load)

    own_load.wait()
    pl.semaphore_wait(barrier, 21)

    started = []

    def send(ref, send_sem, recv_sem, device):
        copy = pltpu.make_async_remote_copy(
            src_ref=ref, dst_ref=ref, send_sem=send_sem, recv_sem=recv_sem,
            device_id=device, device_id_type=MESH,
        )
        copy.start()
        started.append(copy)

    def arrived(ref, send_sem, recv_sem):
        pltpu.make_async_remote_copy(
            src_ref=ref, dst_ref=ref, send_sem=send_sem, recv_sem=recv_sem,
            device_id=sibling, device_id_type=MESH,
        ).wait_recv()

    def rows(dk, dx, which, cc=c):
        return held.at[slot(dk, dx, cc), pl.ds(pl.multiple_of(which * half, half), half), :]

    def lanes(dk, dx, which, side):
        return held.at[
            slot(dk, dx, cc=c),
            pl.ds(pl.multiple_of(which * half, half), half),
            pl.ds(side * (width // 2), width // 2),
        ]

    def share(dk, dx):
        ref = rows(dk, dx, mine)
        send(
            ref, y_send.at[dk, dx], y_recv.at[dk, dx],
            up_y if (dk + dx) % 2 == 0 else down_y,
        )
        send(ref, c_send.at[0, dk, dx], c_recv.at[0, dk, dx], sibling)

    def along_x(dk):
        ref = rows(dk, 0, mine)
        send(ref, x_send.at[dk, 0], x_recv.at[dk, 0], up_x)
        send(ref, x_send.at[dk, 1], x_recv.at[dk, 1], down_x)
        if dk in FAR_DIRECT:
            send(ref, x_send.at[dk, 2], x_recv.at[dk, 2], far_x)

    def relay_x(dk):
        arrived(rows(dk, 3, mine), x_send.at[dk, 0], x_recv.at[dk, 0])
        if dk not in FAR_DIRECT:
            send(lanes(dk, 3, mine, 0), x_send.at[dk, 2], x_recv.at[dk, 2], up_x)
        share(dk, 3)
        arrived(rows(dk, 1, mine), x_send.at[dk, 1], x_recv.at[dk, 1])
        if dk not in FAR_DIRECT:
            send(lanes(dk, 1, mine, 1), x_send.at[dk, 3], x_recv.at[dk, 3], down_x)
        share(dk, 1)

    def finish_x(dk):
        if dk in FAR_DIRECT:
            arrived(rows(dk, 2, mine), x_send.at[dk, 2], x_recv.at[dk, 2])
        else:
            arrived(lanes(dk, 2, mine, 0), x_send.at[dk, 2], x_recv.at[dk, 2])
            arrived(lanes(dk, 2, mine, 1), x_send.at[dk, 3], x_recv.at[dk, 3])
        share(dk, 2)

    def from_y(dk, dxs=(0, 3, 1, 2)):
        for dx in dxs:
            if (dk, dx) == (0, 0):
                continue
            ref = rows(dk, dx, 1 - mine)
            arrived(ref, y_send.at[dk, dx], y_recv.at[dk, dx])
            send(ref, c_send.at[1, dk, dx], c_recv.at[1, dk, dx], sibling)

    def from_sibling(dk):
        for dx in range(4):
            if (dk, dx) == (0, 0):
                arrived(held.at[slot(0, 0, 1 - c)], c_send.at[0, 0, 0], c_recv.at[0, 0, 0])
                continue
            arrived(rows(dk, dx, mine, 1 - c), c_send.at[0, dk, dx], c_recv.at[0, dk, dx])
            arrived(rows(dk, dx, 1 - mine, 1 - c), c_send.at[1, dk, dx], c_recv.at[1, dk, dx])

    def score(dk):
        first = lax.rem(k + dk, 4) * 8

        def score_step(b, carried):
            peak, weight = carried
            tile = lax.dot_general(
                centered[pl.ds(b * SPAN, SPAN)].reshape(SPAN * rowblk, width),
                held[pl.ds(first, 8)].reshape(group, width),
                (((1,), (1,)), ((), ())), preferred_element_type=jnp.float32,
            ) * temper
            scores[dk, pl.ds(b * SPAN, SPAN)] = tile.reshape(SPAN, rowblk, group)
            grouped = tile.reshape(tile.shape[0] // 8, 8, group)
            new_peak = jnp.maximum(peak, jnp.max(grouped, axis=0))
            weight = weight * jnp.exp(peak - new_peak) + jnp.sum(
                jnp.exp(grouped - new_peak[None]), axis=0
            )
            return new_peak, weight

        peak, weight = lax.fori_loop(
            0, nblk // SPAN, score_step,
            (jnp.full((8, group), -jnp.inf, jnp.float32), jnp.zeros((8, group), jnp.float32)),
        )
        top = jnp.max(peak, axis=0, keepdims=True)
        hub = top + jnp.log(jnp.sum(weight * jnp.exp(peak - top), axis=0, keepdims=True))
        for j in range(group // 128):
            hubs[0, pl.ds(lax.rem(k + dk, 4) * (group // 128) + j, 1), :] = hub[
                :, j * 128:(j + 1) * 128
            ]

    send(rows(0, 0, mine), z_send.at[0], z_recv.at[0], up_k)
    send(rows(0, 0, mine), z_send.at[1], z_recv.at[1], down_k)
    along_x(0)
    send(own, c_send.at[0, 0, 0], c_recv.at[0, 0, 0], sibling)

    ids_load.wait()
    centers_load.wait()
    for b in range(nblk):
        loads[b].wait()
        offset = centers[pl.ds(ids[b], 1), :]
        centered[b] = (raw[b].astype(jnp.float32) - offset).astype(jnp.bfloat16)

    relay_x(0)
    arrived(rows(3, 0, mine), z_send.at[0], z_recv.at[0])
    send(lanes(3, 0, mine, 0), z_send.at[2], z_recv.at[2], up_k)
    along_x(3)
    share(3, 0)
    arrived(rows(1, 0, mine), z_send.at[1], z_recv.at[1])
    send(lanes(1, 0, mine, 1), z_send.at[3], z_recv.at[3], down_k)
    along_x(1)
    share(1, 0)
    finish_x(0)
    relay_x(3)
    relay_x(1)
    from_y(0)
    arrived(lanes(2, 0, mine, 0), z_send.at[2], z_recv.at[2])
    arrived(lanes(2, 0, mine, 1), z_send.at[3], z_recv.at[3])
    along_x(2)
    share(2, 0)
    finish_x(3)
    finish_x(1)
    from_sibling(0)
    score(0)
    relay_x(2)
    from_y(3)
    from_y(1)
    finish_x(2)
    from_sibling(3)
    score(3)
    from_y(2)
    from_sibling(1)
    score(1)
    from_sibling(2)
    score(2)

    for stage in range(3):
        me = stage_me[stage]
        for j in SENDS:
            copy = pltpu.make_async_remote_copy(
                src_ref=hubs.at[stage], dst_ref=parts.at[stage, me],
                send_sem=r_send.at[stage, j], recv_sem=r_recv.at[stage, j],
                device_id=stage_peer[stage](j), device_id_type=MESH,
            )
            copy.start()
            started.append(copy)
        parts[stage, me] = hubs[stage]
        for j in range(1, 8):
            arrived(
                parts.at[stage, lax.rem(me + 8 - j, 8)], r_send.at[stage, j], r_recv.at[stage, j]
            )
        every = parts[stage]
        most = jnp.max(every, axis=0)
        hubs[stage + 1] = most + jnp.log(jnp.sum(jnp.exp(every - most[None]), axis=0))

    line = hubs[3, pl.ds(bulk // 4, 1), :]
    quarter = bulk % 4
    own_hub = jnp.zeros((1, piece_rows), jnp.float32)
    for q in range(4):
        own_hub = jnp.where(quarter == q, line[:, q * piece_rows:(q + 1) * piece_rows], own_hub)
    hub_ref[...] = own_hub

    hub_rows = [
        jnp.concatenate(
            [
                hubs[3, pl.ds(lax.rem(k + dk, 4) * (group // 128) + j, 1), :]
                for j in range(group // 128)
            ],
            axis=1,
        )
        for dk in range(4)
    ]
    eye = lax.broadcasted_iota(jnp.int32, (rowblk, rowblk), 0) == lax.broadcasted_iota(
        jnp.int32, (rowblk, rowblk), 1
    )

    def read_step(b, unused):
        tiles = [scores[dk, b] for dk in range(4)]
        adjusted = [2.0 * tiles[dk] - hub_rows[dk] for dk in range(4)]
        most = functools.reduce(jnp.maximum, adjusted)
        most = jnp.max(most, axis=1, keepdims=True)
        weights = [jnp.exp(adjusted[dk] - most) for dk in range(4)]
        summed = jnp.sum(sum(weights), axis=1, keepdims=True)
        matched = jnp.sum(
            sum(weights[dk] * tiles[dk] for dk in range(4)), axis=1, keepdims=True
        )
        logsum = most + jnp.log(summed)
        match = matched / summed
        logsum_ref[pl.ds(b, 1), :] = jnp.sum(jnp.where(eye, logsum, 0.0), axis=0, keepdims=True)
        match_ref[pl.ds(b, 1), :] = jnp.sum(jnp.where(eye, match, 0.0), axis=0, keepdims=True)
        return unused

    lax.fori_loop(0, nblk, read_step, 0)
    for copy in started:
        copy.wait_send()


def hand_out(hub_in, logsum_in, match_in, hub_out, logsum_out, match_out, sems):
    copies = [
        pltpu.make_async_copy(src, dst, sems.at[i])
        for i, (src, dst) in enumerate(
            ((hub_in, hub_out), (logsum_in, logsum_out), (match_in, match_out))
        )
    ]
    for copy in copies:
        copy.start()
    for copy in copies:
        copy.wait()


def per_device(sources, lang_ids, centers, targets):
    rows, width = sources.shape
    nblk = lang_ids.shape[0]
    rowblk = rows // nblk
    piece_rows = targets.shape[0]
    count = 32 * piece_rows
    vmem = pl.BlockSpec(memory_space=pltpu.VMEM)
    dma = pltpu.SemaphoreType.DMA
    hub, logsum, match = pl.pallas_call(
        functools.partial(kernel, rowblk),
        out_shape=(
            jax.ShapeDtypeStruct((1, piece_rows), jnp.float32),
            jax.ShapeDtypeStruct((nblk, rowblk), jnp.float32),
            jax.ShapeDtypeStruct((nblk, rowblk), jnp.float32),
        ),
        in_specs=[pl.BlockSpec(memory_space=pltpu.HBM)] * 4,
        out_specs=(vmem, vmem, vmem),
        scratch_shapes=[
            pltpu.SMEM((nblk,), jnp.int32),
            pltpu.VMEM(centers.shape, jnp.float32),
            pltpu.VMEM((nblk, rowblk, width), jnp.bfloat16),
            pltpu.VMEM((nblk, rowblk, width), jnp.bfloat16),
            pltpu.VMEM((32, piece_rows, width), jnp.bfloat16),
            pltpu.VMEM((4, nblk, rowblk, count // 4), jnp.float32),
            pltpu.VMEM((4, 8, count // 8), jnp.float32),
            pltpu.VMEM((3, 8, 8, count // 8), jnp.float32),
            dma((nblk,)), dma((3,)),
            dma((4,)), dma((4,)),
            dma((4, 4)), dma((4, 4)),
            dma((4, 4)), dma((4, 4)),
            dma((2, 4, 4)), dma((2, 4, 4)),
            dma((3, 8)), dma((3, 8)),
        ],
        compiler_params=pltpu.CompilerParams(
            collective_id=0, has_side_effects=True, vmem_limit_bytes=67043328
        ),
        name="csls",
    )(lang_ids, centers, targets, sources)
    hub, logsum, match = pl.pallas_call(
        hand_out,
        out_shape=tuple(jax.ShapeDtypeStruct(a.shape, a.dtype) for a in (hub, logsum, match)),
        in_specs=[pl.BlockSpec(memory_space=pl.ANY)] * 3,
        out_specs=[pl.BlockSpec(memory_space=pltpu.VMEM)] * 3,
        scratch_shapes=[dma((3,))],
        name="hand_out",
    )(hub, logsum, match)
    return hub.reshape(piece_rows), logsum.reshape(rows), match.reshape(rows)


def solution(mesh):
    in_specs = (P(("lang", "bulk"), None), P(("lang", "bulk")), P(), P("bulk", None))
    out_specs = (P("bulk"), P(("lang", "bulk")), P(("lang", "bulk")))
    return jax.shard_map(
        per_device, mesh=mesh, in_specs=in_specs, out_specs=out_specs, check_vma=False
    )
```

```python
import functools

import jax
import jax.numpy as jnp
from jax import lax
from jax.experimental import pallas as pl
from jax.experimental.pallas import tpu as pltpu
from jax.sharding import PartitionSpec as P

MESH = pl.DeviceIdType.MESH
SENDS = (4, 3, 5, 2, 6, 1, 7)
FAR_DIRECT = (0, 1, 2, 3)
SPAN = 4


def kernel(
    rowblk,
    ids_hbm, centers_hbm, targets_hbm, sources_hbm,
    hub_ref, logsum_ref, match_ref,
    ids, centers, raw, centered, held, scores, hubs, parts,
    load_sem, small_sem,
    z_send, z_recv, x_send, x_recv, y_send, y_recv, c_send, c_recv,
    r_send, r_recv,
):
    lang = lax.axis_index("lang")
    bulk = lax.axis_index("bulk")
    zl, y = lang // 8, lang % 8
    k, x, c = bulk // 8, (bulk // 2) % 4, bulk % 2
    low = bulk % 8
    z = k * 2 + zl
    nblk, _, width = raw.shape
    temper = width ** (-0.5)
    piece_rows = held.shape[1]
    half = piece_rows // 2
    group = 8 * piece_rows
    mine = y % 2

    def at_bulk(kk, xx, cc):
        return (lang, kk * 8 + xx * 2 + cc)

    def slot(dk, dx, cc):
        return lax.rem(k + dk, 4) * 8 + lax.rem(x + dx, 4) * 2 + cc

    up_k = at_bulk(lax.rem(k + 1, 4), x, c)
    down_k = at_bulk(lax.rem(k + 3, 4), x, c)
    up_x = at_bulk(k, lax.rem(x + 1, 4), c)
    down_x = at_bulk(k, lax.rem(x + 3, 4), c)
    far_x = at_bulk(k, lax.rem(x + 2, 4), c)
    up_y = (zl * 8 + lax.rem(y + 1, 8), bulk)
    down_y = (zl * 8 + lax.rem(y + 7, 8), bulk)
    sibling = at_bulk(k, x, 1 - c)

    stage_me = (low, y, z)
    stage_peer = (
        lambda j: (lang, k * 8 + lax.rem(low + j, 8)),
        lambda j: (zl * 8 + lax.rem(y + j, 8), bulk),
        lambda j: (lax.rem(z + j, 2) * 8 + y, (lax.rem(z + j, 8) // 2) * 8 + low),
    )

    barrier = pltpu.get_barrier_semaphore()
    for stage in range(3):
        for j in range(1, 8):
            pl.semaphore_signal(
                barrier, inc=1, device_id=stage_peer[stage](j), device_id_type=MESH
            )

    own = held.at[bulk]
    own_load = pltpu.make_async_copy(targets_hbm, own, small_sem.at[0])
    ids_load = pltpu.make_async_copy(ids_hbm, ids, small_sem.at[1])
    centers_load = pltpu.make_async_copy(centers_hbm, centers, small_sem.at[2])
    own_load.start()
    ids_load.start()
    centers_load.start()
    loads = []
    for b in range(nblk):
        load = pltpu.make_async_copy(
            sources_hbm.at[pl.ds(b * rowblk, rowblk), :], raw.at[b], load_sem.at[b]
        )
        load.start()
        loads.append(load)

    own_load.wait()
    pl.semaphore_wait(barrier, 21)

    started = []

    def send(ref, send_sem, recv_sem, device):
        copy = pltpu.make_async_remote_copy(
            src_ref=ref, dst_ref=ref, send_sem=send_sem, recv_sem=recv_sem,
            device_id=device, device_id_type=MESH,
        )
        copy.start()
        started.append(copy)

    def arrived(ref, send_sem, recv_sem):
        pltpu.make_async_remote_copy(
            src_ref=ref, dst_ref=ref, send_sem=send_sem, recv_sem=recv_sem,
            device_id=sibling, device_id_type=MESH,
        ).wait_recv()

    def rows(dk, dx, which, cc=c):
        return held.at[slot(dk, dx, cc), pl.ds(pl.multiple_of(which * half, half), half), :]

    def lanes(dk, dx, which, side):
        return held.at[
            slot(dk, dx, cc=c),
            pl.ds(pl.multiple_of(which * half, half), half),
            pl.ds(side * (width // 2), width // 2),
        ]

    def share(dk, dx):
        ref = rows(dk, dx, mine)
        send(
            ref, y_send.at[dk, dx], y_recv.at[dk, dx],
            up_y if (dk + dx) % 2 == 0 else down_y,
        )
        send(ref, c_send.at[0, dk, dx], c_recv.at[0, dk, dx], sibling)

    def along_x(dk):
        ref = rows(dk, 0, mine)
        send(ref, x_send.at[dk, 0], x_recv.at[dk, 0], up_x)
        send(ref, x_send.at[dk, 1], x_recv.at[dk, 1], down_x)
        if dk in FAR_DIRECT:
            send(ref, x_send.at[dk, 2], x_recv.at[dk, 2], far_x)

    def relay_x(dk):
        arrived(rows(dk, 3, mine), x_send.at[dk, 0], x_recv.at[dk, 0])
        if dk not in FAR_DIRECT:
            send(lanes(dk, 3, mine, 0), x_send.at[dk, 2], x_recv.at[dk, 2], up_x)
        share(dk, 3)
        arrived(rows(dk, 1, mine), x_send.at[dk, 1], x_recv.at[dk, 1])
        if dk not in FAR_DIRECT:
            send(lanes(dk, 1, mine, 1), x_send.at[dk, 3], x_recv.at[dk, 3], down_x)
        share(dk, 1)

    def finish_x(dk):
        if dk in FAR_DIRECT:
            arrived(rows(dk, 2, mine), x_send.at[dk, 2], x_recv.at[dk, 2])
        else:
            arrived(lanes(dk, 2, mine, 0), x_send.at[dk, 2], x_recv.at[dk, 2])
            arrived(lanes(dk, 2, mine, 1), x_send.at[dk, 3], x_recv.at[dk, 3])
        share(dk, 2)

    def from_y(dk, dxs=(0, 3, 1, 2)):
        for dx in dxs:
            if (dk, dx) == (0, 0):
                continue
            ref = rows(dk, dx, 1 - mine)
            arrived(ref, y_send.at[dk, dx], y_recv.at[dk, dx])
            send(ref, c_send.at[1, dk, dx], c_recv.at[1, dk, dx], sibling)

    def from_sibling(dk):
        for dx in range(4):
            if (dk, dx) == (0, 0):
                arrived(held.at[slot(0, 0, 1 - c)], c_send.at[0, 0, 0], c_recv.at[0, 0, 0])
                continue
            arrived(rows(dk, dx, mine, 1 - c), c_send.at[0, dk, dx], c_recv.at[0, dk, dx])
            arrived(rows(dk, dx, 1 - mine, 1 - c), c_send.at[1, dk, dx], c_recv.at[1, dk, dx])

    def score(dk):
        first = lax.rem(k + dk, 4) * 8

        def score_step(b, carried):
            peak, weight = carried
            tile = lax.dot_general(
                centered[pl.ds(b * SPAN, SPAN)].reshape(SPAN * rowblk, width),
                held[pl.ds(first, 8)].reshape(group, width),
                (((1,), (1,)), ((), ())), preferred_element_type=jnp.float32,
            ) * temper
            scores[dk, pl.ds(b * SPAN, SPAN)] = tile.reshape(SPAN, rowblk, group)
            grouped = tile.reshape(tile.shape[0] // 8, 8, group)
            new_peak = jnp.maximum(peak, jnp.max(grouped, axis=0))
            weight = weight * jnp.exp(peak - new_peak) + jnp.sum(
                jnp.exp(grouped - new_peak[None]), axis=0
            )
            return new_peak, weight

        peak, weight = lax.fori_loop(
            0, nblk // SPAN, score_step,
            (jnp.full((8, group), -jnp.inf, jnp.float32), jnp.zeros((8, group), jnp.float32)),
        )
        top = jnp.max(peak, axis=0, keepdims=True)
        hub = top + jnp.log(jnp.sum(weight * jnp.exp(peak - top), axis=0, keepdims=True))
        for j in range(group // 128):
            hubs[0, pl.ds(lax.rem(k + dk, 4) * (group // 128) + j, 1), :] = hub[
                :, j * 128:(j + 1) * 128
            ]

    send(rows(0, 0, mine), z_send.at[0], z_recv.at[0], up_k)
    send(rows(0, 0, mine), z_send.at[1], z_recv.at[1], down_k)
    along_x(0)
    send(own, c_send.at[0, 0, 0], c_recv.at[0, 0, 0], sibling)

    ids_load.wait()
    centers_load.wait()
    for b in range(nblk):
        loads[b].wait()
        offset = centers[pl.ds(ids[b], 1), :]
        centered[b] = (raw[b].astype(jnp.float32) - offset).astype(jnp.bfloat16)

    relay_x(0)
    arrived(rows(3, 0, mine), z_send.at[0], z_recv.at[0])
    send(lanes(3, 0, mine, 0), z_send.at[2], z_recv.at[2], up_k)
    along_x(3)
    share(3, 0)
    arrived(rows(1, 0, mine), z_send.at[1], z_recv.at[1])
    send(lanes(1, 0, mine, 1), z_send.at[3], z_recv.at[3], down_k)
    along_x(1)
    share(1, 0)
    finish_x(0)
    relay_x(3)
    relay_x(1)
    from_y(0)
    arrived(lanes(2, 0, mine, 0), z_send.at[2], z_recv.at[2])
    arrived(lanes(2, 0, mine, 1), z_send.at[3], z_recv.at[3])
    along_x(2)
    share(2, 0)
    finish_x(3)
    finish_x(1)
    from_sibling(0)
    score(0)
    relay_x(2)
    from_y(3)
    from_y(1)
    finish_x(2)
    from_sibling(3)
    score(3)
    from_y(2)
    from_sibling(1)
    score(1)
    from_sibling(2)
    score(2)

    for stage in range(3):
        me = stage_me[stage]
        for j in SENDS:
            copy = pltpu.make_async_remote_copy(
                src_ref=hubs.at[stage], dst_ref=parts.at[stage, me],
                send_sem=r_send.at[stage, j], recv_sem=r_recv.at[stage, j],
                device_id=stage_peer[stage](j), device_id_type=MESH,
            )
            copy.start()
            started.append(copy)
        parts[stage, me] = hubs[stage]
        for j in range(1, 8):
            arrived(
                parts.at[stage, lax.rem(me + 8 - j, 8)], r_send.at[stage, j], r_recv.at[stage, j]
            )
        every = parts[stage]
        most = jnp.max(every, axis=0)
        hubs[stage + 1] = most + jnp.log(jnp.sum(jnp.exp(every - most[None]), axis=0))

    line = hubs[3, pl.ds(bulk // 4, 1), :]
    quarter = bulk % 4
    own_hub = jnp.zeros((1, piece_rows), jnp.float32)
    for q in range(4):
        own_hub = jnp.where(quarter == q, line[:, q * piece_rows:(q + 1) * piece_rows], own_hub)
    hub_ref[...] = own_hub

    hub_rows = [
        jnp.concatenate(
            [
                hubs[3, pl.ds(lax.rem(k + dk, 4) * (group // 128) + j, 1), :]
                for j in range(group // 128)
            ],
            axis=1,
        )
        for dk in range(4)
    ]
    eye = lax.broadcasted_iota(jnp.int32, (rowblk, rowblk), 0) == lax.broadcasted_iota(
        jnp.int32, (rowblk, rowblk), 1
    )

    def read_step(b, unused):
        tiles = [scores[dk, b] for dk in range(4)]
        adjusted = [2.0 * tiles[dk] - hub_rows[dk] for dk in range(4)]
        most = functools.reduce(jnp.maximum, adjusted)
        most = jnp.max(most, axis=1, keepdims=True)
        weights = [jnp.exp(adjusted[dk] - most) for dk in range(4)]
        summed = jnp.sum(sum(weights), axis=1, keepdims=True)
        matched = jnp.sum(
            sum(weights[dk] * tiles[dk] for dk in range(4)), axis=1, keepdims=True
        )
        logsum = most + jnp.log(summed)
        match = matched / summed
        logsum_ref[pl.ds(b, 1), :] = jnp.sum(jnp.where(eye, logsum, 0.0), axis=0, keepdims=True)
        match_ref[pl.ds(b, 1), :] = jnp.sum(jnp.where(eye, match, 0.0), axis=0, keepdims=True)
        return unused

    lax.fori_loop(0, nblk, read_step, 0, unroll=2)
    for copy in started:
        copy.wait_send()


def hand_out(hub_in, logsum_in, match_in, hub_out, logsum_out, match_out, sems):
    copies = [
        pltpu.make_async_copy(src, dst, sems.at[i])
        for i, (src, dst) in enumerate(
            ((hub_in, hub_out), (logsum_in, logsum_out), (match_in, match_out))
        )
    ]
    for copy in copies:
        copy.start()
    for copy in copies:
        copy.wait()


def per_device(sources, lang_ids, centers, targets):
    rows, width = sources.shape
    nblk = lang_ids.shape[0]
    rowblk = rows // nblk
    piece_rows = targets.shape[0]
    count = 32 * piece_rows
    vmem = pl.BlockSpec(memory_space=pltpu.VMEM)
    dma = pltpu.SemaphoreType.DMA
    hub, logsum, match = pl.pallas_call(
        functools.partial(kernel, rowblk),
        out_shape=(
            jax.ShapeDtypeStruct((1, piece_rows), jnp.float32),
            jax.ShapeDtypeStruct((nblk, rowblk), jnp.float32),
            jax.ShapeDtypeStruct((nblk, rowblk), jnp.float32),
        ),
        in_specs=[pl.BlockSpec(memory_space=pltpu.HBM)] * 4,
        out_specs=(vmem, vmem, vmem),
        scratch_shapes=[
            pltpu.SMEM((nblk,), jnp.int32),
            pltpu.VMEM(centers.shape, jnp.float32),
            pltpu.VMEM((nblk, rowblk, width), jnp.bfloat16),
            pltpu.VMEM((nblk, rowblk, width), jnp.bfloat16),
            pltpu.VMEM((32, piece_rows, width), jnp.bfloat16),
            pltpu.VMEM((4, nblk, rowblk, count // 4), jnp.float32),
            pltpu.VMEM((4, 8, count // 8), jnp.float32),
            pltpu.VMEM((3, 8, 8, count // 8), jnp.float32),
            dma((nblk,)), dma((3,)),
            dma((4,)), dma((4,)),
            dma((4, 4)), dma((4, 4)),
            dma((4, 4)), dma((4, 4)),
            dma((2, 4, 4)), dma((2, 4, 4)),
            dma((3, 8)), dma((3, 8)),
        ],
        compiler_params=pltpu.CompilerParams(
            collective_id=0, has_side_effects=True, vmem_limit_bytes=67043328
        ),
        name="csls",
    )(lang_ids, centers, targets, sources)
    hub, logsum, match = pl.pallas_call(
        hand_out,
        out_shape=tuple(jax.ShapeDtypeStruct(a.shape, a.dtype) for a in (hub, logsum, match)),
        in_specs=[pl.BlockSpec(memory_space=pl.ANY)] * 3,
        out_specs=[pl.BlockSpec(memory_space=pltpu.VMEM)] * 3,
        scratch_shapes=[dma((3,))],
        name="hand_out",
    )(hub, logsum, match)
    return hub.reshape(piece_rows), logsum.reshape(rows), match.reshape(rows)


def solution(mesh):
    in_specs = (P(("lang", "bulk"), None), P(("lang", "bulk")), P(), P("bulk", None))
    out_specs = (P("bulk"), P(("lang", "bulk")), P(("lang", "bulk")))
    return jax.shard_map(
        per_device, mesh=mesh, in_specs=in_specs, out_specs=out_specs, check_vma=False
    )
```
